256 devices in a mesh: dp: 16 (over y, x), tensor: 16 (over z, core).
Axes of the slice: x: 4, y: 4, z: 8, core: 2. Of those that a mesh axis runs over, the one named last changes fastest.
Arguments:
- residual: bfloat16 [1792, 4096], P('dp'), may hold values from -6 to 6
- x_in: bfloat16 [1792, 8192], P('dp', 'tensor'), may hold values from -6 to 6
- z_in: bfloat16 [1792, 8192], P('dp', 'tensor'), may hold values from -6 to 6
- conv_state: bfloat16 [3, 1792, 8192], P(None, 'dp', 'tensor'), may hold values from -6 to 6
- conv_weight: float32 [4, 8192], P(None, 'tensor'), may hold values from -3 to 3
- conv_bias: float32 [8192], P('tensor'), may hold values from -3 to 3
- xproj_weight: bfloat16 [8192, 288], P('tensor'), may hold values from -0.0625 to 0.0625
- dtproj_weight: bfloat16 [256, 8192], P(None, 'tensor'), may hold values from -0.375 to 0.375
- dt_bias: float32 [8192], P('tensor'), may hold values from -4 to -1
- a_log: float32 [16, 8192], P(None, 'tensor'), may hold values from 0 to 2.8
- skip_d: float32 [8192], P('tensor'), may hold values from 0.5 to 1.5
- ssm_state: bfloat16 [1792, 16, 8192], P('dp', None, 'tensor'), may hold values from -6 to 6
- out_weight: bfloat16 [8192, 4096], P('tensor'), may hold values from -0.0625 to 0.0625
- norm_gain: float32 [4096], replicated, may hold values from 0.5 to 1.5
- head_weight: bfloat16 [65024, 4096], P(('dp', 'tensor')), may hold values from -80 to 80, as said below
Outputs:
- logprobs: bfloat16 [1792, 65024], P(None, ('dp', 'tensor'))
- state_next: bfloat16 [1792, 16, 8192], P('dp', None, 'tensor')
The draws below stay inside these ranges and needn't reach their ends.
Inputs may be any that keep to these rules, and one draw needn't show every extreme that they name: `head_weight`: rows of the output embedding.
All inputs are finite; a program needn't handle non-finite values.
Results may differ from the reference program's by a relative error of at most 0.008.
Values may be sent and summed in bfloat16 or wider, within the bound.
A program may use at most 128 MiB of HBM per device.

```python
import math
import jax
import jax.numpy as jnp
from jax import lax

D = 4096
DI = 8192
NSTATE = 16
RANK = 256
CONV = 4
VOCAB = 65024
SEQS = 1792


def draw_head_weight(key, part):
    base_key = jax.random.fold_in(jax.random.fold_in(key, 17), 0)
    table = jnp.clip(jax.random.normal(base_key, (VOCAB, D), jnp.float32), -6.0, 6.0) * (3.0 / math.sqrt(D))
    return table.astype(jnp.bfloat16)


def levels(key, extent, shards, smallest, high):
    factor_of, own = 1.0, jax.random.fold_in(key, 6)
    for axis_at, parts in shards:
        steps = jnp.exp(jax.random.uniform(jax.random.fold_in(own, axis_at), (parts,), jnp.float32, smallest / len(shards), high / len(shards)))
        factor_of = factor_of * jnp.repeat(steps, extent[axis_at] // parts).reshape([-1 if axis == axis_at else 1 for axis in range(len(extent))])
    return factor_of


def gaussian(key, extent, scale, bound, cuts=(), kind=jnp.bfloat16):
    drawn = jax.random.normal(key, extent, jnp.float32) * scale
    if len(cuts) > 0:
        drawn = levels(key, extent, cuts, -0.22, 0.18) * drawn
    return jnp.clip(drawn, min=-bound, max=bound).astype(kind)


def setup_inputs(seed: int = 0) -> dict:
    arg_keys = jax.random.split(jax.random.key(seed), 16)
    return {
        "residual": gaussian(arg_keys[0], (SEQS, D), 1.0, 6.0, ((0, 16),)),
        "x_in": gaussian(arg_keys[1], (SEQS, DI), 1.0, 6.0, ((0, 16), (1, 16))),
        "z_in": gaussian(arg_keys[2], (SEQS, DI), 1.0, 6.0, ((0, 16), (1, 16))),
        "conv_state": gaussian(arg_keys[3], (CONV - 1, SEQS, DI), 1.0, 6.0, ((1, 16), (2, 16))),
        "conv_weight": gaussian(arg_keys[4], (CONV, DI), CONV ** -0.5, 3.0, ((1, 16),), jnp.float32),
        "conv_bias": gaussian(arg_keys[5], (DI,), 0.5, 3.0, ((0, 16),), jnp.float32),
        "xproj_weight": gaussian(arg_keys[6], (DI, RANK + 2 * NSTATE), DI ** -0.5, 0.0625, ((0, 16),)),
        "dtproj_weight": gaussian(arg_keys[7], (RANK, DI), RANK ** -0.5, 0.375, ((1, 16),)),
        "dt_bias": jnp.clip(-4.0 + 3.0 * jax.random.uniform(arg_keys[8], (DI,), jnp.float32) ** levels(arg_keys[8], (DI,), ((0, 16),), -0.2, 0.2), -4.0, -1.0),
        "a_log": jnp.clip(2.8 * jax.random.uniform(arg_keys[9], (NSTATE, DI), jnp.float32) ** levels(arg_keys[9], (NSTATE, DI), ((1, 16),), -0.2, 0.2), 0.0, 2.8),
        "skip_d": jnp.clip(0.5 + 1.0 * jax.random.uniform(arg_keys[10], (DI,), jnp.float32) ** levels(arg_keys[10], (DI,), ((0, 16),), -0.2, 0.2), 0.5, 1.5),
        "ssm_state": gaussian(arg_keys[11], (SEQS, NSTATE, DI), 1.0, 6.0, ((0, 16), (2, 16))),
        "out_weight": gaussian(arg_keys[12], (DI, D), DI ** -0.5, 0.0625, ((0, 16),)),
        "norm_gain": jnp.clip(1.0 + 0.1 * jax.random.normal(arg_keys[13], (D,), jnp.float32), 0.5, 1.5),
        "head_weight": draw_head_weight(jax.random.fold_in(arg_keys[15], 71), 0),
    }


def rms_scale(values, epsilon):
    return values * lax.rsqrt(lax.optimization_barrier(jnp.mean(values * values, axis=-1, keepdims=True)) + epsilon)

def reference(residual, x_in, z_in, conv_state, conv_weight, conv_bias, xproj_weight, dtproj_weight, dt_bias, a_log, skip_d, ssm_state, out_weight, norm_gain, head_weight):
    window = jnp.concatenate([conv_state.astype(jnp.float32), x_in.astype(jnp.float32)[None]], axis=0)
    conv_out = lax.optimization_barrier(jnp.sum(window * conv_weight[:, None, :], axis=0)) + conv_bias
    mixed_x = jax.nn.silu(conv_out).astype(jnp.bfloat16)
    projected = jnp.dot(mixed_x, xproj_weight, preferred_element_type=jnp.float32)
    rate_low = rms_scale(projected[:, :RANK], 1e-06).astype(jnp.bfloat16)
    input_coef = rms_scale(projected[:, RANK:RANK + NSTATE], 1e-06)
    output_coef = rms_scale(projected[:, RANK + NSTATE:], 1e-06)
    step_size = jax.nn.softplus(jnp.dot(rate_low, dtproj_weight, preferred_element_type=jnp.float32) + dt_bias)
    conv_value = mixed_x.astype(jnp.float32)
    decay_rate = jnp.exp(step_size[:, None, :] * (-jnp.exp(a_log))[None])
    state_new = decay_rate * ssm_state.astype(jnp.float32) + (step_size * conv_value)[:, None, :] * input_coef[:, :, None]
    ssm_out = lax.optimization_barrier(jnp.sum(state_new * output_coef[:, :, None], axis=1)) + skip_d * conv_value
    gated_out = (ssm_out * jax.nn.silu(z_in.astype(jnp.float32))).astype(jnp.bfloat16)
    hidden = residual.astype(jnp.float32) + jnp.dot(gated_out, out_weight, preferred_element_type=jnp.float32)
    normed = (rms_scale(hidden, 1e-05) * norm_gain).astype(jnp.bfloat16)
    logits = lax.dot_general(normed, head_weight, (((1,), (1,)), ((), ())), preferred_element_type=jnp.float32)
    row_max = lax.optimization_barrier(jnp.max(logits, axis=1, keepdims=True))
    log_total = row_max + jnp.log(lax.optimization_barrier(jnp.sum(jnp.exp(logits - row_max), axis=1, keepdims=True)))
    return ((logits - log_total).astype(jnp.bfloat16), state_new.astype(jnp.bfloat16))
```

```python
import jax
import jax.numpy as jnp
from jax import lax
from jax.experimental import pallas as pl
from jax.experimental.pallas import tpu as pltpu
from jax.sharding import Mesh
from jax.sharding import PartitionSpec as P

NSTATE = 16
RANK = 256
TENSOR = ("tensor_0", "tensor_1")
DP = ("dp_0", "dp_1")
DP_TENSOR = ("dp_0", "dp_1", "tensor_0", "tensor_1")

D = 4096
HALF = D // 2
PIECE = 256
CH = 512
ROWS = 112
VOC = 254
VPAD = 256
NY, NX, NZ, NC = 4, 4, 8, 2
NDP, NT = NY * NX, NZ * NC
TOP = 32
LOW = ROWS - TOP
F32 = jnp.float32
BF16 = jnp.bfloat16
NT_DIMS = (((1,), (1,)), ((), ()))


class Wires:
    def __init__(self, send_sem, recv_sem):
        self.send_sem, self.recv_sem, self.used, self.live = send_sem, recv_sem, 0, []

    def send(self, src, dst, device):
        at = self.used
        self.used += 1
        copy = pltpu.make_async_remote_copy(
            src_ref=src,
            dst_ref=dst,
            send_sem=self.send_sem.at[at],
            recv_sem=self.recv_sem.at[at],
            device_id=device,
            device_id_type=pl.DeviceIdType.MESH,
        )
        copy.start()
        self.live.append(copy)
        return copy

    def close(self):
        for copy in self.live:
            copy.wait_send()


def wrap(value, size):
    return lax.rem(value + size, size)


def diagonal(rows):
    shape = (rows, 128)
    return lax.broadcasted_iota(jnp.int32, shape, 0) == lax.broadcasted_iota(jnp.int32, shape, 1)


def log_add(values):
    top = values[0]
    for value in values[1:]:
        top = jnp.maximum(top, value)
    total = jnp.exp(values[0] - top)
    for value in values[1:]:
        total = total + jnp.exp(value - top)
    return top + jnp.log(total)


def head_kernel(
    gated_ref,
    out_w,
    head_w,
    resid,
    gain_ref,
    out_ref,
    wo,
    raw,
    wh,
    gx,
    res,
    inv_gain,
    rs_send,
    rs_recv,
    buf,
    own,
    part,
    got,
    lse_own,
    lse_t,
    lse_mid,
    lse_d,
    send_sem,
    recv_sem,
    local_sem,
):
    y, x = lax.axis_index("dp_0"), lax.axis_index("dp_1")
    z, c = lax.axis_index("tensor_0"), lax.axis_index("tensor_1")
    mate = 1 - c
    wires = Wires(send_sem, recv_sem)

    def dev(yy=None, xx=None, zz=None, cc=None):
        return tuple(a if b is None else b for a, b in ((y, yy), (x, xx), (z, zz), (c, cc)))

    t, d = z * NC + c, y * NX + x
    tensor_mates = []
    for off in range(1, NT):
        other = wrap(t + off, NT)
        tensor_mates.append(dev(zz=other // NC, cc=lax.rem(other, NC)))
    dp_mates = []
    for off in range(1, NDP):
        other = wrap(d + off, NDP)
        dp_mates.append(dev(yy=other // NX, xx=lax.rem(other, NX)))

    mine = pl.ds(pl.multiple_of(c * HALF, HALF), HALF)
    theirs = pl.ds(pl.multiple_of(mate * HALF, HALF), HALF)
    feature = pl.ds(pl.multiple_of(c * HALF + z * PIECE, PIECE), PIECE)
    local = [
        pltpu.make_async_copy(out_w.at[:, mine], wo.at[c], local_sem.at[0]),
        pltpu.make_async_copy(head_w.at[:, mine], raw.at[c], local_sem.at[1]),
        pltpu.make_async_copy(resid.at[:, feature], res, local_sem.at[2]),
    ]
    for copy in local:
        copy.start()

    barrier = pltpu.get_barrier_semaphore()
    for other in tensor_mates + dp_mates:
        pl.semaphore_signal(
            barrier, inc=1, device_id=other, device_id_type=pl.DeviceIdType.MESH
        )
    pl.semaphore_wait(barrier, len(tensor_mates) + len(dp_mates))

    sibling = dev(cc=mate)
    gx_copy = wires.send(gated_ref, gx.at[c], sibling)
    wo_copy = wires.send(out_w.at[:, theirs], wo.at[c], sibling)
    wh_copy = wires.send(head_w.at[:, theirs], raw.at[c], sibling)

    gains = gain_ref[pl.ds(pl.multiple_of(c * NZ, NZ), NZ), :]
    inv_gain[...] = 1.0 / (gains * gains)

    local[0].wait()
    gx_copy.wait_recv()
    wo_copy.wait_recv()
    halves = (gated_ref[...], gx[mate])
    rs_copies = {}
    for off in (4, 3, 5, 2, 6, 1, 7, 0):
        target = wrap(z + off, NZ)
        columns = pl.ds(pl.multiple_of(target * PIECE, PIECE), PIECE)
        block = jnp.dot(halves[0], wo[c, :, columns], preferred_element_type=F32) + jnp.dot(
            halves[1], wo[mate, :, columns], preferred_element_type=F32
        )
        if off:
            rs_send[off] = block.astype(BF16)
            rs_copies[off] = wires.send(rs_send.at[off], rs_recv.at[off], dev(zz=target))
    local[2].wait()
    hidden = block + res[...].astype(F32)
    for off in (7, 1, 6, 2, 5, 3, 4):
        rs_copies[off].wait_recv()
        hidden = hidden + rs_recv[off].astype(F32)
    gain = gain_ref[pl.ds(c * NZ + z, 1), :]
    buf[y, x, z] = (hidden * gain).astype(BF16)

    top, low = pl.ds(0, TOP), pl.ds(TOP, LOW)
    left_cols, right_cols = pl.ds(0, 128), pl.ds(128, 128)

    def same(ref, device):
        return wires.send(ref, ref, device)

    class Ring4:
        def __init__(self, at, me, device_of):
            self.at, self.me, self.device_of = at, me, device_of

        def start(self):
            up, down = self.device_of(wrap(self.me + 1, 4)), self.device_of(wrap(self.me + 3, 4))
            self.up0 = same(self.at(self.me, 0), up)
            self.down1 = same(self.at(self.me, 1), down)
            self.up1 = same(self.at(self.me, 1), up)
            self.down0 = same(self.at(self.me, 0), down)

        def forward(self):
            up, down = wrap(self.me + 1, 4), wrap(self.me + 3, 4)
            self.up0.wait_recv()
            self.far0 = same(self.at(down, 0), self.device_of(up))
            self.down1.wait_recv()
            self.far1 = same(self.at(up, 1), self.device_of(down))

        def near(self):
            self.up1.wait_recv()
            self.down0.wait_recv()

        def far(self):
            self.far0.wait_recv()
            self.far1.wait_recv()

    def at_y(yy):
        return dev(yy=yy)

    def at_x(xx):
        return dev(xx=xx)

    def at_z(zz):
        return dev(zz=zz)

    def half(size, h):
        return pl.ds(h * (size // 2), size // 2)

    top_y = [
        same(buf.at[y, x, z, top, :], at_y(wrap(y + off, NY))) for off in (2, 1, 3)
    ]
    low_z = [
        same(buf.at[y, x, z, low, :], at_z(wrap(z + off, NZ))) for off in (4, 3, 5, 2, 6, 1, 7)
    ]
    local[1].wait()
    wh_copy.wait_recv()
    for k in range(NC):
        wh[k, VPAD - 16 :, :] = jnp.zeros((16, HALF), BF16)
        wh[k, :VOC, :] = raw[k]
    for copy in top_y:
        copy.wait_recv()
    top_x = [
        same(buf.at[:, x, z, top, :], at_x(wrap(x + off, NX))) for off in (2, 1, 3)
    ]
    left_y = Ring4(lambda i, h: buf.at[i, x, half(NZ, h), low, left_cols], y, at_y)
    right_x = Ring4(lambda i, h: buf.at[y, i, half(NZ, h), low, right_cols], x, at_x)
    left_x = Ring4(lambda i, h: buf.at[half(NY, h), i, :, low, left_cols], x, at_x)
    right_y = Ring4(lambda i, h: buf.at[i, half(NX, h), :, low, right_cols], y, at_y)
    for copy in low_z:
        copy.wait_recv()
    left_y.start()
    right_x.start()
    for copy in top_x:
        copy.wait_recv()

    def slab(i):
        return buf.at[:, :, wrap(i, NZ), top, :]

    def half_slab(i, h):
        return buf.at[half(NY, h), :, wrap(i, NZ), top, :]

    z_up, z_down = at_z(wrap(z + 1, NZ)), at_z(wrap(z - 1, NZ))
    up = same(slab(z), z_up)
    down = same(slab(z), z_down)
    left_y.forward()
    right_x.forward()
    left_y.near()
    right_x.near()
    up.wait_recv()
    up = same(slab(z - 1), z_up)
    down.wait_recv()
    down = same(slab(z + 1), z_down)
    left_y.far()
    left_x.start()
    right_x.far()
    right_y.start()
    up.wait_recv()
    up = same(slab(z - 2), z_up)
    down.wait_recv()
    down = same(slab(z + 2), z_down)
    left_x.forward()
    right_y.forward()
    up.wait_recv()
    up = same(half_slab(z - 3, 0), z_up)
    down.wait_recv()
    down = same(half_slab(z + 3, 1), z_down)

    lane = lax.broadcasted_iota(jnp.int32, (1, VPAD), 1)

    def partial_logits(lhs, rows, store):
        values = jnp.concatenate(lhs, axis=1)
        power = jnp.zeros((rows, PIECE), F32)
        for k in range(NZ):
            wide = lhs[k].astype(F32)
            power = power + wide * wide * inv_gain[k : k + 1, :]
        power = jnp.sum(power, axis=1, keepdims=True)
        store(part, jnp.where(
            lane == VOC, power, lax.dot_general(values, wh[mate], NT_DIMS, preferred_element_type=F32)
        ))
        store(own, jnp.where(
            lane == VOC, power, lax.dot_general(values, wh[c], NT_DIMS, preferred_element_type=F32)
        ))

    up.wait_recv()
    down.wait_recv()
    top_swaps = []
    for yy in range(NY):
        lhs = [buf[yy, :, k, 0:TOP, :].reshape(NX * TOP, PIECE) for k in range(NZ)]

        def store(ref, value, yy=yy):
            ref[yy * NX : (yy + 1) * NX, 0:TOP, :] = value.reshape(NX, TOP, VPAD)

        partial_logits(lhs, NX * TOP, store)
        at = pl.ds(yy * NX, NX)
        top_swaps.append(wires.send(part.at[at, top, :], got.at[at, top, :], sibling))

    def low_blocks(blocks):
        lhs = [
            jnp.concatenate([buf[yy, xx, k, TOP:ROWS, :] for yy, xx in blocks], axis=0)
            for k in range(NZ)
        ]

        def store(ref, value):
            for i, (yy, xx) in enumerate(blocks):
                ref[yy * NX + xx, TOP:ROWS, :] = value[i * LOW : (i + 1) * LOW, :]

        partial_logits(lhs, len(blocks) * LOW, store)
        swaps = []
        for yy, xx in blocks:
            at = yy * NX + xx
            swaps.append(wires.send(part.at[at, low, :], got.at[at, low, :], sibling))
        return swaps

    def finish(blocks, swaps):
        for copy in swaps:
            copy.wait_recv()
        for yy, xx in blocks:
            at = yy * NX + xx
            total = own[at] + got[at]
            scale = lax.rsqrt(total[:, VOC : VOC + 1] / D + 1e-05)
            logits = total * scale
            own[at] = logits
            held = jnp.where(lane < VOC, logits, -jnp.inf)
            peak = jnp.max(held, axis=1, keepdims=True)
            mass = jnp.sum(jnp.exp(held - peak), axis=1, keepdims=True)
            spread = jnp.where(diagonal(ROWS), peak + jnp.log(mass), 0.0)
            lse_own[pl.ds(at, 1), :] = jnp.sum(spread, axis=0, keepdims=True)

    near_y, near_x = [y, wrap(y + 1, NY), wrap(y + 3, NY)], [x, wrap(x + 1, NX), wrap(x + 3, NX)]
    far_y, far_x = wrap(y + 2, NY), wrap(x + 2, NX)
    left_x.near()
    right_y.near()
    groups = [[(yy, xx) for yy in near_y] for xx in near_x]
    swaps = [low_blocks(blocks) for blocks in groups]
    left_x.far()
    right_y.far()
    last = [[(yy, far_x) for yy in near_y + [far_y]], [(far_y, xx) for xx in near_x]]
    for copy in top_swaps:
        copy.wait_recv()
    swaps.append(low_blocks(last[0]))
    for blocks, held in zip(groups, swaps):
        finish(blocks, held)
    swaps.append(low_blocks(last[1]))
    finish(last[0], swaps[-2])
    finish(last[1], swaps[-1])

    rounds = [
        wires.send(lse_own, lse_t.at[i], other) for i, other in enumerate(tensor_mates)
    ]
    for copy in rounds:
        copy.wait_recv()
    lse_mid[...] = log_add([lse_own[...]] + [lse_t[i] for i in range(NT - 1)])
    rounds = [wires.send(lse_mid, lse_d.at[i], other) for i, other in enumerate(dp_mates)]
    for copy in rounds:
        copy.wait_recv()
    lse_own_total = log_add([lse_mid[...]] + [lse_d[i] for i in range(NDP - 1)])
    for at in range(NDP):
        row = jnp.broadcast_to(lse_own_total[at : at + 1, :], (ROWS, 128))
        column = jnp.sum(jnp.where(diagonal(ROWS), row, 0.0), axis=1, keepdims=True)
        out_ref[at * ROWS : (at + 1) * ROWS, :] = (own[at] - column)[:, :VOC].astype(BF16)
    wires.close()


N_WIRES = 160


def head(gated, out_w, head_w, resid, gain):
    vmem = pl.BlockSpec(memory_space=pltpu.VMEM)
    hbm = pl.BlockSpec(memory_space=pl.ANY)
    return pl.pallas_call(
        head_kernel,
        out_shape=jax.ShapeDtypeStruct((NDP * ROWS, VOC), BF16),
        in_specs=[vmem, hbm, hbm, hbm, vmem],
        out_specs=vmem,
        scratch_shapes=[
            pltpu.VMEM((NC, CH, HALF), BF16),
            pltpu.VMEM((NC, VOC, HALF), BF16),
            pltpu.VMEM((NC, VPAD, HALF), BF16),
            pltpu.VMEM((NC, ROWS, CH), BF16),
            pltpu.VMEM((ROWS, PIECE), BF16),
            pltpu.VMEM((NZ, PIECE), F32),
            pltpu.VMEM((NZ, ROWS, PIECE), BF16),
            pltpu.VMEM((NZ, ROWS, PIECE), BF16),
            pltpu.VMEM((NY, NX, NZ, ROWS, PIECE), BF16),
            pltpu.VMEM((NDP, ROWS, VPAD), F32),
            pltpu.VMEM((NDP, ROWS, VPAD), F32),
            pltpu.VMEM((NDP, ROWS, VPAD), F32),
            pltpu.VMEM((NDP, 128), F32),
            pltpu.VMEM((NT - 1, NDP, 128), F32),
            pltpu.VMEM((NDP, 128), F32),
            pltpu.VMEM((NDP - 1, NDP, 128), F32),
            pltpu.SemaphoreType.DMA((N_WIRES,)),
            pltpu.SemaphoreType.DMA((N_WIRES,)),
            pltpu.SemaphoreType.DMA((3,)),
        ],
        compiler_params=pltpu.CompilerParams(
            collective_id=0, has_side_effects=True, vmem_limit_bytes=50 * 2**20
        ),
        name="head",
    )(gated, out_w, head_w, resid, gain.reshape(D // PIECE, PIECE))


def rms_scale(values, epsilon):
    return values * lax.rsqrt(jnp.mean(values * values, axis=-1, keepdims=True) + epsilon)


def on_device(
    residual,
    x_in,
    z_in,
    conv_state,
    conv_weight,
    conv_bias,
    xproj_weight,
    dtproj_weight,
    dt_bias,
    a_log,
    skip_d,
    ssm_state,
    out_weight,
    norm_gain,
    head_weight,
):
    window = jnp.concatenate(
        [conv_state.astype(jnp.float32), x_in.astype(jnp.float32)[None]], axis=0
    )
    conv_out = jnp.sum(window * conv_weight[:, None, :], axis=0) + conv_bias
    mixed_x = jax.nn.silu(conv_out).astype(jnp.bfloat16)
    partial_value = jnp.dot(mixed_x, xproj_weight, preferred_element_type=jnp.float32)
    projected = lax.all_gather(partial_value, TENSOR).sum(0)
    rate_low = rms_scale(projected[:, :RANK], 1e-06).astype(jnp.bfloat16)
    input_coef = rms_scale(projected[:, RANK : RANK + NSTATE], 1e-06)
    output_coef = rms_scale(projected[:, RANK + NSTATE :], 1e-06)
    step_size = jax.nn.softplus(
        jnp.dot(rate_low, dtproj_weight, preferred_element_type=jnp.float32) + dt_bias
    )
    conv_value = mixed_x.astype(jnp.float32)
    decay_rate = jnp.exp(step_size[:, None, :] * (-jnp.exp(a_log))[None])
    state_new = (
        decay_rate * ssm_state.astype(jnp.float32)
        + (step_size * conv_value)[:, None, :] * input_coef[:, :, None]
    )
    ssm_out = jnp.sum(state_new * output_coef[:, :, None], axis=1) + skip_d * conv_value
    gated_out = (ssm_out * jax.nn.silu(z_in.astype(jnp.float32))).astype(jnp.bfloat16)
    logprobs = head(gated_out, out_weight, head_weight, residual, norm_gain)
    return (logprobs, state_new.astype(jnp.bfloat16))


def solution(mesh):
    torus = Mesh(mesh.devices.reshape(4, 4, 8, 2), ("dp_0", "dp_1", "tensor_0", "tensor_1"))
    placed = (
        P(DP, None),
        P(DP, TENSOR),
        P(DP, TENSOR),
        P(None, DP, TENSOR),
        P(None, TENSOR),
        P(TENSOR),
        P(TENSOR, None),
        P(None, TENSOR),
        P(TENSOR),
        P(None, TENSOR),
        P(TENSOR),
        P(DP, None, TENSOR),
        P(TENSOR, None),
        P(),
        P(DP_TENSOR, None),
    )
    return jax.shard_map(
        on_device,
        mesh=torus,
        in_specs=placed,
        out_specs=(P(None, DP_TENSOR), P(DP, None, TENSOR)),
        check_vma=False,
    )
```

```python
import jax
import jax.numpy as jnp
from jax import lax
from jax.experimental import pallas as pl
from jax.experimental.pallas import tpu as pltpu
from jax.sharding import Mesh
from jax.sharding import PartitionSpec as P

NSTATE = 16
RANK = 256
TENSOR = ("tensor_0", "tensor_1")
DP = ("dp_0", "dp_1")
DP_TENSOR = ("dp_0", "dp_1", "tensor_0", "tensor_1")

D = 4096
HALF = D // 2
PIECE = 256
CH = 512
ROWS = 112
VOC = 254
VPAD = 256
NY, NX, NZ, NC = 4, 4, 8, 2
NDP, NT = NY * NX, NZ * NC
OWN = ROWS // NT
PROJ = RANK + 2 * NSTATE
TOP = 32
LOW = ROWS - TOP
F32 = jnp.float32
BF16 = jnp.bfloat16
NT_DIMS = (((1,), (1,)), ((), ()))


class Wires:
    def __init__(self, send_sem, recv_sem):
        self.send_sem, self.recv_sem, self.used, self.live = send_sem, recv_sem, 0, []

    def send(self, src, dst, device):
        at = self.used
        self.used += 1
        copy = pltpu.make_async_remote_copy(
            src_ref=src,
            dst_ref=dst,
            send_sem=self.send_sem.at[at],
            recv_sem=self.recv_sem.at[at],
            device_id=device,
            device_id_type=pl.DeviceIdType.MESH,
        )
        copy.start()
        self.live.append(copy)
        return copy

    def close(self):
        for copy in self.live:
            copy.wait_send()


def wrap(value, size):
    return lax.rem(value + size, size)


def diagonal(rows):
    shape = (rows, 128)
    return lax.broadcasted_iota(jnp.int32, shape, 0) == lax.broadcasted_iota(jnp.int32, shape, 1)


def log_add(values):
    top = values[0]
    for value in values[1:]:
        top = jnp.maximum(top, value)
    total = jnp.exp(values[0] - top)
    for value in values[1:]:
        total = total + jnp.exp(value - top)
    return top + jnp.log(total)


def wide_row(ref):
    return jnp.concatenate([ref[i : i + 1, :] for i in range(ref.shape[0])], axis=1)


def softplus(value):
    return jnp.maximum(value, 0.0) + jnp.log1p(jnp.exp(-jnp.abs(value)))


def silu(value):
    return value * jax.nn.sigmoid(value)


def step_kernel(*refs):
    (
        resid,
        x_in,
        z_in,
        conv_state,
        conv_w,
        conv_b,
        xproj_w,
        dtproj_w,
        dt_b,
        a_log,
        skip_d,
        ssm_state,
        out_w,
        norm_gain,
        head_w,
        out_ref,
        state_ref,
        v_xin,
        v_zin,
        v_conv,
        v_convw,
        v_convb,
        v_xproj,
        v_dtproj,
        v_dtb,
        v_alog,
        v_skip,
        v_state,
        gain_ref,
        new_state,
        mixed,
        proj,
        p_send,
        p_recv,
        scaled,
        step,
        result,
        wo,
        raw,
        wh,
        gx,
        res,
        inv_gain,
        rs_send,
        rs_recv,
        buf,
        own,
        part,
        got,
        lse_own,
        lse_t,
        lse_mid,
        lse_d,
        send_sem,
        recv_sem,
        local_sem,
    ) = refs
    y, x = lax.axis_index("dp_0"), lax.axis_index("dp_1")
    z, c = lax.axis_index("tensor_0"), lax.axis_index("tensor_1")
    mate = 1 - c
    wires = Wires(send_sem, recv_sem)

    def dev(yy=None, xx=None, zz=None, cc=None):
        return tuple(a if b is None else b for a, b in ((y, yy), (x, xx), (z, zz), (c, cc)))

    t, d = z * NC + c, y * NX + x
    tensor_mates, mate_at = [], []
    for off in range(1, NT):
        other = wrap(t + off, NT)
        mate_at.append(other)
        tensor_mates.append(dev(zz=other // NC, cc=lax.rem(other, NC)))
    dp_mates = []
    for off in range(1, NDP):
        other = wrap(d + off, NDP)
        dp_mates.append(dev(yy=other // NX, xx=lax.rem(other, NX)))
    sibling = dev(cc=mate)

    mine = pl.ds(pl.multiple_of(c * HALF, HALF), HALF)
    theirs = pl.ds(pl.multiple_of(mate * HALF, HALF), HALF)
    feature = pl.ds(pl.multiple_of(c * HALF + z * PIECE, PIECE), PIECE)
    local = {}

    def fetch(name, src, dst):
        local[name] = pltpu.make_async_copy(src, dst, local_sem.at[len(local)])
        local[name].start()

    barrier = pltpu.get_barrier_semaphore()
    for other in tensor_mates + dp_mates:
        pl.semaphore_signal(
            barrier, inc=1, device_id=other, device_id_type=pl.DeviceIdType.MESH
        )
    fetch("convw", conv_w, v_convw)
    fetch("convb", conv_b, v_convb)
    fetch("xin", x_in, v_xin)
    fetch("conv", conv_state, v_conv)
    fetch("xproj", xproj_w, v_xproj)
    fetch("dtproj", dtproj_w, v_dtproj)
    fetch("dtb", dt_b, v_dtb)
    fetch("alog", a_log, v_alog)
    fetch("skip", skip_d, v_skip)
    fetch("state", ssm_state, v_state)
    fetch("zin", z_in, v_zin)
    fetch("gain", norm_gain, gain_ref)
    fetch("res", resid.at[:, feature], res)
    fetch("wo", out_w.at[:, mine], wo.at[c])
    fetch("wh", head_w.at[:, mine], raw.at[c])

    for name in ("convw", "convb", "xin", "conv"):
        local[name].wait()
    conv = v_xin[...].astype(F32) * v_convw[3:4, :]
    for k in range(3):
        conv = conv + v_conv[k].astype(F32) * v_convw[k : k + 1, :]
    mixed[...] = silu(conv + wide_row(v_convb)).astype(BF16)
    local["xproj"].wait()
    proj[0:ROWS, :] = lax.dot_general(
        mixed[...], v_xproj[...], NT_DIMS, preferred_element_type=F32
    )
    proj[ROWS:, :] = jnp.zeros((8, PROJ), F32)
    for k in range(NT):
        p_send[k] = proj[OWN * k : OWN * k + 8, :].astype(BF16)
    pl.semaphore_wait(barrier, len(tensor_mates) + len(dp_mates))

    rounds = [
        wires.send(p_send.at[at], p_recv.at[i], other)
        for i, (at, other) in enumerate(zip(mate_at, tensor_mates))
    ]
    total = p_send[t].astype(F32)
    for i, copy in enumerate(rounds):
        copy.wait_recv()
        total = total + p_recv[i].astype(F32)
    column = lax.broadcasted_iota(jnp.int32, (1, PROJ), 1)
    power = total * total
    scale = jnp.zeros((8, PROJ), F32)
    for first, size in ((0, RANK), (RANK, NSTATE), (RANK + NSTATE, NSTATE)):
        inside = (column >= first) & (column < first + size)
        mean = jnp.sum(jnp.where(inside, power, 0.0), axis=1, keepdims=True) / size
        scale = jnp.where(inside, lax.rsqrt(mean + 1e-06), scale)
    scaled[t] = (total * scale).astype(BF16)
    rounds = [wires.send(scaled.at[t], scaled.at[t], other) for other in tensor_mates]
    wo_copy = wires.send(out_w.at[:, theirs], wo.at[c], sibling)
    for name in ("dtproj", "dtb", "alog", "skip", "state", "zin", "gain"):
        local[name].wait()
    rates = -jnp.exp(v_alog[...])
    skip = wide_row(v_skip)
    for copy in rounds:
        copy.wait_recv()
    for k in range(NT):
        proj[OWN * k : OWN * k + 8, :] = scaled[k].astype(F32)

    step[...] = softplus(
        jnp.dot(proj[0:ROWS, 0:RANK].astype(BF16), v_dtproj[...], preferred_element_type=F32)
        + wide_row(v_dtb)
    )
    low_eye = lax.broadcasted_iota(jnp.int32, (NSTATE, 2 * NSTATE), 1) - lax.broadcasted_iota(
        jnp.int32, (NSTATE, 2 * NSTATE), 0
    )

    def some_rows(i, carry):
        at = pl.ds(pl.multiple_of(i * 16, 16), 16)
        delta, mixed_x = step[at, :], mixed[at, :].astype(F32)
        pushed = delta * mixed_x
        coefs = proj[at, RANK:PROJ]
        sums = []
        for j in range(16):
            row = jnp.broadcast_to(coefs[j : j + 1, :], (NSTATE, 2 * NSTATE))
            in_col = jnp.sum(jnp.where(low_eye == 0, row, 0.0), axis=1, keepdims=True)
            out_col = jnp.sum(jnp.where(low_eye == NSTATE, row, 0.0), axis=1, keepdims=True)
            new = (
                jnp.exp(delta[j : j + 1, :] * rates) * v_state[i * 16 + j].astype(F32)
                + in_col * pushed[j : j + 1, :]
            )
            new_state[i * 16 + j] = new.astype(BF16)
            sums.append(jnp.sum(new * out_col, axis=0, keepdims=True))
        value = jnp.concatenate(sums, axis=0) + skip * mixed_x
        gx[c, at, :] = (value * silu(v_zin[at, :].astype(F32))).astype(BF16)
        return carry

    lax.fori_loop(0, ROWS // 16, some_rows, 0)
    gx_copy = wires.send(gx.at[c], gx.at[c], sibling)
    wh_copy = wires.send(head_w.at[:, theirs], raw.at[c], sibling)
    state_out = pltpu.make_async_copy(new_state, state_ref, local_sem.at[len(local)])
    state_out.start()

    gain_rows = 2 * NZ
    gains = gain_ref[pl.ds(pl.multiple_of(c * gain_rows, gain_rows), gain_rows), :]
    inv_gain[...] = 1.0 / (gains * gains)

    local["wo"].wait()
    wo_copy.wait_recv()
    gx_copy.wait_recv()
    halves = (gx[c], gx[mate])
    rs_copies = {}
    for off in (4, 3, 5, 2, 6, 1, 7, 0):
        target = wrap(z + off, NZ)
        columns = pl.ds(pl.multiple_of(target * PIECE, PIECE), PIECE)
        block = jnp.dot(halves[0], wo[c, :, columns], preferred_element_type=F32) + jnp.dot(
            halves[1], wo[mate, :, columns], preferred_element_type=F32
        )
        if off:
            rs_send[off] = block.astype(BF16)
            rs_copies[off] = wires.send(rs_send.at[off], rs_recv.at[off], dev(zz=target))
    local["res"].wait()
    hidden = block + res[...].astype(F32)
    for off in (7, 1, 6, 2, 5, 3, 4):
        rs_copies[off].wait_recv()
        hidden = hidden + rs_recv[off].astype(F32)
    gain = jnp.concatenate(
        [gain_ref[pl.ds((c * NZ + z) * 2 + i, 1), :] for i in range(2)], axis=1
    )
    buf[y, x, z] = (hidden * gain).astype(BF16)

    top, low = pl.ds(0, TOP), pl.ds(TOP, LOW)
    left_cols, right_cols = pl.ds(0, 128), pl.ds(128, 128)

    def same(ref, device):
        return wires.send(ref, ref, device)

    class Ring4:
        def __init__(self, at, me, device_of):
            self.at, self.me, self.device_of = at, me, device_of

        def start(self):
            up, down = self.device_of(wrap(self.me + 1, 4)), self.device_of(wrap(self.me + 3, 4))
            self.up0 = same(self.at(self.me, 0), up)
            self.down1 = same(self.at(self.me, 1), down)
            self.up1 = same(self.at(self.me, 1), up)
            self.down0 = same(self.at(self.me, 0), down)

        def forward(self):
            up, down = wrap(self.me + 1, 4), wrap(self.me + 3, 4)
            self.up0.wait_recv()
            self.far0 = same(self.at(down, 0), self.device_of(up))
            self.down1.wait_recv()
            self.far1 = same(self.at(up, 1), self.device_of(down))

        def near(self):
            self.up1.wait_recv()
            self.down0.wait_recv()

        def far(self):
            self.far0.wait_recv()
            self.far1.wait_recv()

    def at_y(yy):
        return dev(yy=yy)

    def at_x(xx):
        return dev(xx=xx)

    def at_z(zz):
        return dev(zz=zz)

    def half(size, h):
        return pl.ds(h * (size // 2), size // 2)

    top_y = [
        same(buf.at[y, x, z, top, :], at_y(wrap(y + off, NY))) for off in (2, 1, 3)
    ]
    low_z = [
        same(buf.at[y, x, z, low, :], at_z(wrap(z + off, NZ))) for off in (4, 3, 5, 2, 6, 1, 7)
    ]
    local["wh"].wait()
    wh_copy.wait_recv()
    for k in range(NC):
        wh[k, VPAD - 16 :, :] = jnp.zeros((16, HALF), BF16)
        wh[k, :VOC, :] = raw[k]
    for copy in top_y:
        copy.wait_recv()
    top_x = [
        same(buf.at[:, x, z, top, :], at_x(wrap(x + off, NX))) for off in (2, 1, 3)
    ]
    left_y = Ring4(lambda i, h: buf.at[i, x, half(NZ, h), low, left_cols], y, at_y)
    right_x = Ring4(lambda i, h: buf.at[y, i, half(NZ, h), low, right_cols], x, at_x)
    left_x = Ring4(lambda i, h: buf.at[half(NY, h), i, :, low, left_cols], x, at_x)
    right_y = Ring4(lambda i, h: buf.at[i, half(NX, h), :, low, right_cols], y, at_y)
    for copy in low_z:
        copy.wait_recv()
    left_y.start()
    right_x.start()
    for copy in top_x:
        copy.wait_recv()

    def slab(i):
        return buf.at[:, :, wrap(i, NZ), top, :]

    def half_slab(i, h):
        return buf.at[half(NY, h), :, wrap(i, NZ), top, :]

    z_up, z_down = at_z(wrap(z + 1, NZ)), at_z(wrap(z - 1, NZ))
    up = same(slab(z), z_up)
    down = same(slab(z), z_down)
    left_y.forward()
    right_x.forward()
    left_y.near()
    right_x.near()
    up.wait_recv()
    up = same(slab(z - 1), z_up)
    down.wait_recv()
    down = same(slab(z + 1), z_down)
    left_y.far()
    left_x.start()
    right_x.far()
    right_y.start()
    up.wait_recv()
    up = same(slab(z - 2), z_up)
    down.wait_recv()
    down = same(slab(z + 2), z_down)
    left_x.forward()
    right_y.forward()
    up.wait_recv()
    up = same(half_slab(z - 3, 0), z_up)
    down.wait_recv()
    down = same(half_slab(z + 3, 1), z_down)

    lane = lax.broadcasted_iota(jnp.int32, (1, VPAD), 1)

    def partial_logits(lhs, rows, store):
        values = jnp.concatenate(lhs, axis=1)
        power = jnp.zeros((rows, PIECE), F32)
        for k in range(NZ):
            wide = lhs[k].astype(F32)
            power = power + wide * wide * wide_row(inv_gain.at[2 * k : 2 * k + 2, :])
        power = jnp.sum(power, axis=1, keepdims=True)
        store(part, jnp.where(
            lane == VOC, power, lax.dot_general(values, wh[mate], NT_DIMS, preferred_element_type=F32)
        ))
        store(own, jnp.where(
            lane == VOC, power, lax.dot_general(values, wh[c], NT_DIMS, preferred_element_type=F32)
        ))

    up.wait_recv()
    down.wait_recv()
    top_swaps = []
    for yy in range(NY):
        lhs = [buf[yy, :, k, 0:TOP, :].reshape(NX * TOP, PIECE) for k in range(NZ)]

        def store(ref, value, yy=yy):
            ref[yy * NX : (yy + 1) * NX, 0:TOP, :] = value.reshape(NX, TOP, VPAD)

        partial_logits(lhs, NX * TOP, store)
        at = pl.ds(yy * NX, NX)
        top_swaps.append(wires.send(part.at[at, top, :], got.at[at, top, :], sibling))

    def low_blocks(blocks):
        lhs = [
            jnp.concatenate([buf[yy, xx, k, TOP:ROWS, :] for yy, xx in blocks], axis=0)
            for k in range(NZ)
        ]

        def store(ref, value):
            for i, (yy, xx) in enumerate(blocks):
                ref[yy * NX + xx, TOP:ROWS, :] = value[i * LOW : (i + 1) * LOW, :]

        partial_logits(lhs, len(blocks) * LOW, store)
        swaps = []
        for yy, xx in blocks:
            at = yy * NX + xx
            swaps.append(wires.send(part.at[at, low, :], got.at[at, low, :], sibling))
        return swaps

    def finish(blocks, swaps):
        for copy in swaps:
            copy.wait_recv()
        for yy, xx in blocks:
            at = yy * NX + xx
            total = own[at] + got[at]
            scale = lax.rsqrt(total[:, VOC : VOC + 1] / D + 1e-05)
            logits = total * scale
            own[at] = logits
            held = jnp.where(lane < VOC, logits, -jnp.inf)
            peak = jnp.max(held, axis=1, keepdims=True)
            mass = jnp.sum(jnp.exp(held - peak), axis=1, keepdims=True)
            spread = jnp.where(diagonal(ROWS), peak + jnp.log(mass), 0.0)
            lse_own[pl.ds(at, 1), :] = jnp.sum(spread, axis=0, keepdims=True)

    near_y, near_x = [y, wrap(y + 1, NY), wrap(y + 3, NY)], [x, wrap(x + 1, NX), wrap(x + 3, NX)]
    far_y, far_x = wrap(y + 2, NY), wrap(x + 2, NX)
    left_x.near()
    right_y.near()
    groups = [[(yy, xx) for yy in near_y] for xx in near_x]
    swaps = [low_blocks(blocks) for blocks in groups]
    left_x.far()
    right_y.far()
    last = [[(yy, far_x) for yy in near_y + [far_y]], [(far_y, xx) for xx in near_x]]
    for copy in top_swaps:
        copy.wait_recv()
    swaps.append(low_blocks(last[0]))
    for blocks, held in zip(groups, swaps):
        finish(blocks, held)
    swaps.append(low_blocks(last[1]))
    finish(last[0], swaps[-2])
    finish(last[1], swaps[-1])

    rounds = [
        wires.send(lse_own, lse_t.at[i], other) for i, other in enumerate(tensor_mates)
    ]
    for copy in rounds:
        copy.wait_recv()
    lse_mid[...] = log_add([lse_own[...]] + [lse_t[i] for i in range(NT - 1)])
    rounds = [wires.send(lse_mid, lse_d.at[i], other) for i, other in enumerate(dp_mates)]
    for copy in rounds:
        copy.wait_recv()
    lse_own_total = log_add([lse_mid[...]] + [lse_d[i] for i in range(NDP - 1)])
    outs = []
    for at in range(NDP):
        row = jnp.broadcast_to(lse_own_total[at : at + 1, :], (ROWS, 128))
        column = jnp.sum(jnp.where(diagonal(ROWS), row, 0.0), axis=1, keepdims=True)
        block = slice(at * ROWS, (at + 1) * ROWS)
        result[block, :] = (own[at] - column)[:, :VOC].astype(BF16)
        outs.append(
            pltpu.make_async_copy(
                result.at[block, :], out_ref.at[block, :], local_sem.at[len(local) + 1 + at]
            )
        )
        outs[-1].start()
    for copy in outs + [state_out]:
        copy.wait()
    wires.close()


N_WIRES = 200


def step_call(args):
    hbm = pl.BlockSpec(memory_space=pl.ANY)
    return pl.pallas_call(
        step_kernel,
        out_shape=(
            jax.ShapeDtypeStruct((NDP * ROWS, VOC), BF16),
            jax.ShapeDtypeStruct((ROWS, NSTATE, CH), BF16),
        ),
        in_specs=[hbm] * len(args),
        out_specs=(hbm, hbm),
        scratch_shapes=[
            pltpu.VMEM((ROWS, CH), BF16),
            pltpu.VMEM((ROWS, CH), BF16),
            pltpu.VMEM((3, ROWS, CH), BF16),
            pltpu.VMEM((4, CH), F32),
            pltpu.VMEM((4, 128), F32),
            pltpu.VMEM((PROJ, CH), BF16),
            pltpu.VMEM((RANK, CH), BF16),
            pltpu.VMEM((4, 128), F32),
            pltpu.VMEM((NSTATE, CH), F32),
            pltpu.VMEM((4, 128), F32),
            pltpu.VMEM((ROWS, NSTATE, CH), BF16),
            pltpu.VMEM((D // 128, 128), F32),
            pltpu.VMEM((ROWS, NSTATE, CH), BF16),
            pltpu.VMEM((ROWS, CH), BF16),
            pltpu.VMEM((ROWS + 8, PROJ), F32),
            pltpu.VMEM((NT, 8, PROJ), BF16),
            pltpu.VMEM((NT - 1, 8, PROJ), BF16),
            pltpu.VMEM((NT, 8, PROJ), BF16),
            pltpu.VMEM((ROWS, CH), F32),
            pltpu.VMEM((NDP * ROWS, VOC), BF16),
            pltpu.VMEM((NC, CH, HALF), BF16),
            pltpu.VMEM((NC, VOC, HALF), BF16),
            pltpu.VMEM((NC, VPAD, HALF), BF16),
            pltpu.VMEM((NC, ROWS, CH), BF16),
            pltpu.VMEM((ROWS, PIECE), BF16),
            pltpu.VMEM((2 * NZ, 128), F32),
            pltpu.VMEM((NZ, ROWS, PIECE), BF16),
            pltpu.VMEM((NZ, ROWS, PIECE), BF16),
            pltpu.VMEM((NY, NX, NZ, ROWS, PIECE), BF16),
            pltpu.VMEM((NDP, ROWS, VPAD), F32),
            pltpu.VMEM((NDP, ROWS, VPAD), F32),
            pltpu.VMEM((NDP, ROWS, VPAD), F32),
            pltpu.VMEM((NDP, 128), F32),
            pltpu.VMEM((NT - 1, NDP, 128), F32),
            pltpu.VMEM((NDP, 128), F32),
            pltpu.VMEM((NDP - 1, NDP, 128), F32),
            pltpu.SemaphoreType.DMA((N_WIRES,)),
            pltpu.SemaphoreType.DMA((N_WIRES,)),
            pltpu.SemaphoreType.DMA((40,)),
        ],
        compiler_params=pltpu.CompilerParams(
            collective_id=0, has_side_effects=True, vmem_limit_bytes=56 * 2**20
        ),
        name="step",
    )(*args)


def on_device(
    residual,
    x_in,
    z_in,
    conv_state,
    conv_weight,
    conv_bias,
    xproj_weight,
    dtproj_weight,
    dt_bias,
    a_log,
    skip_d,
    ssm_state,
    out_weight,
    norm_gain,
    head_weight,
):
    return step_call(
        (
            residual,
            x_in,
            z_in,
            conv_state,
            conv_weight,
            conv_bias.reshape(-1, 128),
            xproj_weight.T,
            dtproj_weight,
            dt_bias.reshape(-1, 128),
            a_log,
            skip_d.reshape(-1, 128),
            ssm_state,
            out_weight,
            norm_gain.reshape(-1, 128),
            head_weight,
        )
    )


def solution(mesh):
    torus = Mesh(mesh.devices.reshape(4, 4, 8, 2), ("dp_0", "dp_1", "tensor_0", "tensor_1"))
    placed = (
        P(DP, None),
        P(DP, TENSOR),
        P(DP, TENSOR),
        P(None, DP, TENSOR),
        P(None, TENSOR),
        P(TENSOR),
        P(TENSOR, None),
        P(None, TENSOR),
        P(TENSOR),
        P(None, TENSOR),
        P(TENSOR),
        P(DP, None, TENSOR),
        P(TENSOR, None),
        P(),
        P(DP_TENSOR, None),
    )
    return jax.shard_map(
        on_device,
        mesh=torus,
        in_specs=placed,
        out_specs=(P(None, DP_TENSOR), P(DP, None, TENSOR)),
        check_vma=False,
    )
```

```python
import jax
import jax.numpy as jnp
from jax import lax
from jax.experimental import pallas as pl
from jax.experimental.pallas import tpu as pltpu
from jax.sharding import Mesh
from jax.sharding import PartitionSpec as P

NSTATE = 16
RANK = 256
TENSOR = ("tensor_0", "tensor_1")
DP = ("dp_0", "dp_1")
DP_TENSOR = ("dp_0", "dp_1", "tensor_0", "tensor_1")

D = 4096
HALF = D // 2
PIECE = 256
CH = 512
ROWS = 112
VOC = 254
VPAD = 256
NY, NX, NZ, NC = 4, 4, 8, 2
NDP, NT = NY * NX, NZ * NC
OWN = ROWS // NT
PROJ = RANK + 2 * NSTATE
FIRST, MIDDLE, LAST = (0, 48), (48, 32), (80, 32)
EARLY = LAST[0]
PER_ROW = 128 // LAST[1]
F32 = jnp.float32
BF16 = jnp.bfloat16
NT_DIMS = (((1,), (1,)), ((), ()))


class Wires:
    def __init__(self, send_sem, recv_sem):
        self.send_sem, self.recv_sem, self.used, self.live = send_sem, recv_sem, 0, []

    def send(self, src, dst, device):
        at = self.used
        self.used += 1
        copy = pltpu.make_async_remote_copy(
            src_ref=src,
            dst_ref=dst,
            send_sem=self.send_sem.at[at],
            recv_sem=self.recv_sem.at[at],
            device_id=device,
            device_id_type=pl.DeviceIdType.MESH,
        )
        copy.start()
        self.live.append(copy)
        return copy

    def close(self):
        for copy in self.live:
            copy.wait_send()


def wrap(value, size):
    return lax.rem(value + size, size)


def log_add(values):
    top = values[0]
    for value in values[1:]:
        top = jnp.maximum(top, value)
    total = jnp.exp(values[0] - top)
    for value in values[1:]:
        total = total + jnp.exp(value - top)
    return top + jnp.log(total)


def wide_row(ref):
    return jnp.concatenate([ref[i : i + 1, :] for i in range(ref.shape[0])], axis=1)


def softplus(value):
    return jnp.maximum(value, 0.0) + jnp.log1p(jnp.exp(-jnp.abs(value)))


def silu(value):
    return value * jax.nn.sigmoid(value)


def step_kernel(*refs):
    (
        resid,
        x_in,
        z_in,
        conv_state,
        conv_w,
        conv_b,
        xproj_w,
        dtproj_w,
        dt_b,
        a_log,
        skip_d,
        ssm_state,
        out_w,
        norm_gain,
        head_w,
        out_ref,
        state_ref,
        v_xin,
        v_zin,
        v_conv,
        v_convw,
        v_convb,
        v_xproj,
        v_dtproj,
        v_dtb,
        v_alog,
        v_skip,
        v_state,
        gain_ref,
        mixed,
        proj,
        p_send,
        p_recv,
        scaled,
        step,
        wo,
        raw,
        wh,
        gx,
        res,
        inv_gain,
        rs_send,
        rs_recv,
        buf,
        own,
        part,
        got,
        lse_own,
        lse_t,
        lse_mid,
        lse_d,
        late_own,
        late_t,
        late_mid,
        late_d,
        hidden,
        new_state,
        result,
        wt,
        send_sem,
        recv_sem,
        local_sem,
    ) = refs
    y, x = lax.axis_index("dp_0"), lax.axis_index("dp_1")
    z, c = lax.axis_index("tensor_0"), lax.axis_index("tensor_1")
    mate = 1 - c
    wires = Wires(send_sem, recv_sem)

    def dev(yy=None, xx=None, zz=None, cc=None):
        return tuple(a if b is None else b for a, b in ((y, yy), (x, xx), (z, zz), (c, cc)))

    t, d = z * NC + c, y * NX + x
    tensor_mates, mate_at = [], []
    for off in range(1, NT):
        other = wrap(t + off, NT)
        mate_at.append(other)
        tensor_mates.append(dev(zz=other // NC, cc=lax.rem(other, NC)))
    dp_mates = []
    for off in range(1, NDP):
        other = wrap(d + off, NDP)
        dp_mates.append(dev(yy=other // NX, xx=lax.rem(other, NX)))
    sibling = dev(cc=mate)

    mine = pl.ds(pl.multiple_of(c * HALF, HALF), HALF)
    theirs = pl.ds(pl.multiple_of(mate * HALF, HALF), HALF)
    feature = pl.ds(pl.multiple_of(c * HALF + z * PIECE, PIECE), PIECE)
    local = {}

    def fetch(name, src, dst):
        local[name] = pltpu.make_async_copy(src, dst, local_sem.at[len(local)])
        local[name].start()

    barrier = pltpu.get_barrier_semaphore()
    for other in tensor_mates + dp_mates:
        pl.semaphore_signal(
            barrier, inc=1, device_id=other, device_id_type=pl.DeviceIdType.MESH
        )
    fetch("convw", conv_w, v_convw)
    fetch("convb", conv_b, v_convb)
    fetch("xin", x_in, v_xin)
    fetch("conv", conv_state, v_conv)
    fetch("xproj", xproj_w, v_xproj)
    fetch("dtproj", dtproj_w, v_dtproj)
    fetch("dtb", dt_b, v_dtb)
    fetch("alog", a_log, v_alog)
    fetch("skip", skip_d, v_skip)
    fetch("state", ssm_state, v_state)
    fetch("zin", z_in, v_zin)
    fetch("gain", norm_gain, gain_ref)
    fetch("res", resid.at[:, feature], res)
    fetch("wo", out_w.at[:, mine], wo.at[c])
    fetch("wh", head_w.at[:, mine], raw.at[c])

    for name in ("convw", "convb", "xin", "conv"):
        local[name].wait()
    conv = v_xin[...].astype(F32) * v_convw[3:4, :]
    for k in range(3):
        conv = conv + v_conv[k].astype(F32) * v_convw[k : k + 1, :]
    mixed[...] = silu(conv + wide_row(v_convb)).astype(BF16)
    local["xproj"].wait()
    proj[0:ROWS, :] = lax.dot_general(
        mixed[...], v_xproj[...], NT_DIMS, preferred_element_type=F32
    )
    proj[ROWS:, :] = jnp.zeros((8, PROJ), F32)
    for k in range(NT):
        p_send[k] = proj[OWN * k : OWN * k + 8, :].astype(BF16)
    pl.semaphore_wait(barrier, len(tensor_mates) + len(dp_mates))

    rounds = [
        wires.send(p_send.at[at], p_recv.at[i], other)
        for i, (at, other) in enumerate(zip(mate_at, tensor_mates))
    ]
    total = p_send[t].astype(F32)
    for i, copy in enumerate(rounds):
        copy.wait_recv()
        total = total + p_recv[i].astype(F32)
    column = lax.broadcasted_iota(jnp.int32, (1, PROJ), 1)
    power = total * total
    scale = jnp.zeros((8, PROJ), F32)
    for first, size in ((0, RANK), (RANK, NSTATE), (RANK + NSTATE, NSTATE)):
        inside = (column >= first) & (column < first + size)
        mean = jnp.sum(jnp.where(inside, power, 0.0), axis=1, keepdims=True) / size
        scale = jnp.where(inside, lax.rsqrt(mean + 1e-06), scale)
    scaled[t] = (total * scale).astype(BF16)
    rounds = [wires.send(scaled.at[t], scaled.at[t], other) for other in tensor_mates]
    wo_copy = wires.send(out_w.at[:, theirs], wo.at[c], sibling)
    for name in ("dtproj", "dtb", "alog", "skip", "state", "zin", "gain"):
        local[name].wait()
    rates = -jnp.exp(v_alog[...])
    skip = wide_row(v_skip)
    for copy in rounds:
        copy.wait_recv()
    for k in range(NT):
        proj[OWN * k : OWN * k + 8, :] = scaled[k].astype(F32)

    step[...] = softplus(
        jnp.dot(proj[0:ROWS, 0:RANK].astype(BF16), v_dtproj[...], preferred_element_type=F32)
        + wide_row(v_dtb)
    )
    low_eye = lax.broadcasted_iota(jnp.int32, (NSTATE, 2 * NSTATE), 1) - lax.broadcasted_iota(
        jnp.int32, (NSTATE, 2 * NSTATE), 0
    )

    def some_rows(i, carry):
        at = pl.ds(pl.multiple_of(i * 16, 16), 16)
        delta, mixed_x = step[at, :], mixed[at, :].astype(F32)
        pushed = delta * mixed_x
        coefs = proj[at, RANK:PROJ]
        sums = []
        for j in range(16):
            row = jnp.broadcast_to(coefs[j : j + 1, :], (NSTATE, 2 * NSTATE))
            in_col = jnp.sum(jnp.where(low_eye == 0, row, 0.0), axis=1, keepdims=True)
            out_col = jnp.sum(jnp.where(low_eye == NSTATE, row, 0.0), axis=1, keepdims=True)
            new = (
                jnp.exp(delta[j : j + 1, :] * rates) * v_state[i * 16 + j].astype(F32)
                + in_col * pushed[j : j + 1, :]
            )
            new_state[i * 16 + j] = new.astype(BF16)
            sums.append(jnp.sum(new * out_col, axis=0, keepdims=True))
        value = jnp.concatenate(sums, axis=0) + skip * mixed_x
        gx[c, at, :] = (value * silu(v_zin[at, :].astype(F32))).astype(BF16)
        return carry

    split = FIRST[1]
    chunks = (pl.ds(0, split), pl.ds(split, ROWS - split))
    lax.fori_loop(0, split // 16, some_rows, 0)
    gx_copies = [wires.send(gx.at[c, chunks[0], :], gx.at[c, chunks[0], :], sibling)]
    lax.fori_loop(split // 16, ROWS // 16, some_rows, 0)
    gx_copies.append(wires.send(gx.at[c, chunks[1], :], gx.at[c, chunks[1], :], sibling))
    wh_copy = wires.send(head_w.at[:, theirs], raw.at[c], sibling)
    outs = []

    def leave(src, dst):
        outs.append(pltpu.make_async_copy(src, dst, local_sem.at[len(local) + len(outs)]))
        outs[-1].start()

    leave(new_state, state_ref)

    gain_rows = 2 * NZ
    gains = gain_ref[pl.ds(pl.multiple_of(c * gain_rows, gain_rows), gain_rows), :]
    inv_gain[...] = 1.0 / (gains * gains)

    local["wo"].wait()
    wo_copy.wait_recv()
    rs_copies = [{}, {}]
    for chunk, rows in enumerate(chunks):
        gx_copies[chunk].wait_recv()
        halves = (gx[c, rows, :], gx[mate, rows, :])
        for off in (4, 3, 5, 2, 6, 1, 7, 0):
            target = wrap(z + off, NZ)
            columns = pl.ds(pl.multiple_of(target * PIECE, PIECE), PIECE)
            block = jnp.dot(halves[0], wo[c, :, columns], preferred_element_type=F32) + jnp.dot(
                halves[1], wo[mate, :, columns], preferred_element_type=F32
            )
            if off:
                rs_send[off, rows, :] = block.astype(BF16)
                rs_copies[chunk][off] = wires.send(
                    rs_send.at[off, rows, :], rs_recv.at[off, rows, :], dev(zz=target)
                )
        hidden[rows, :] = block
    local["res"].wait()
    gain = jnp.concatenate(
        [gain_ref[pl.ds((c * NZ + z) * 2 + i, 1), :] for i in range(2)], axis=1
    )

    def reduce_over_z(chunk):
        rows = chunks[chunk]
        value = hidden[rows, :] + res[rows, :].astype(F32)
        for off in (7, 1, 6, 2, 5, 3, 4):
            rs_copies[chunk][off].wait_recv()
            value = value + rs_recv[off, rows, :].astype(F32)
        value = (value * gain).astype(BF16)
        for h in range(2):
            buf[y, x, z, h, rows, :] = value[:, h * 128 : (h + 1) * 128]

    first, middle, last = (pl.ds(*rows) for rows in (FIRST, MIDDLE, LAST))

    def same(ref, device):
        return wires.send(ref, ref, device)

    class Ring4:
        def __init__(self, at, me, device_of):
            self.at, self.me, self.device_of = at, me, device_of

        def start(self):
            up, down = self.device_of(wrap(self.me + 1, 4)), self.device_of(wrap(self.me + 3, 4))
            self.up0 = same(self.at(self.me, 0), up)
            self.down1 = same(self.at(self.me, 1), down)
            self.up1 = same(self.at(self.me, 1), up)
            self.down0 = same(self.at(self.me, 0), down)

        def forward(self):
            up, down = wrap(self.me + 1, 4), wrap(self.me + 3, 4)
            self.up0.wait_recv()
            self.far0 = same(self.at(down, 0), self.device_of(up))
            self.down1.wait_recv()
            self.far1 = same(self.at(up, 1), self.device_of(down))

        def near(self):
            self.up1.wait_recv()
            self.down0.wait_recv()

        def far(self):
            self.far0.wait_recv()
            self.far1.wait_recv()

    def at_y(yy):
        return dev(yy=yy)

    def at_x(xx):
        return dev(xx=xx)

    def at_z(zz):
        return dev(zz=zz)

    def half(size, h):
        return pl.ds(h * (size // 2), size // 2)

    def over_z(rows):
        return [
            same(buf.at[y, x, z, :, rows, :], at_z(wrap(z + off, NZ))) for off in (4, 3, 5, 2, 6, 1, 7)
        ]

    def arrived(copies):
        for copy in copies:
            copy.wait_recv()

    def rings(rows):
        return (
            Ring4(lambda i, h: buf.at[i, x, half(NZ, h), 0, rows, :], y, at_y),
            Ring4(lambda i, h: buf.at[y, i, half(NZ, h), 1, rows, :], x, at_x),
            Ring4(lambda i, h: buf.at[half(NY, h), i, :, 0, rows, :], x, at_x),
            Ring4(lambda i, h: buf.at[i, half(NX, h), :, 1, rows, :], y, at_y),
        )

    z_up, z_down = at_z(wrap(z + 1, NZ)), at_z(wrap(z - 1, NZ))

    def slab(i, h):
        return buf.at[half(NY, h), :, wrap(i, NZ), :, middle, :]

    def along_z(step):
        ups, downs = slabs[-1] if step else (None, None)
        now = ([], [])
        for h in range(2):
            if step:
                ups[h].wait_recv()
            if step < NZ // 2 - 1 or h == 0:
                now[0].append(same(slab(z - step, h), z_up))
            if step:
                downs[1 - h].wait_recv()
            if step < NZ // 2 - 1 or h == 0:
                now[1].insert(0, same(slab(z + step, 1 - h), z_down))
        slabs.append(now)

    slabs = []
    left_y0, right_x0, left_x0, right_y0 = rings(first)
    left_y1, right_x1, left_x1, right_y1 = rings(last)

    reduce_over_z(0)
    first_z = over_z(first)
    reduce_over_z(1)
    middle_y = [same(buf.at[y, x, z, :, middle, :], at_y(wrap(y + off, NY))) for off in (2, 1, 3)]
    last_z = over_z(last)
    local["wh"].wait()
    wh_copy.wait_recv()
    for k in range(NC):
        wh[k, VPAD - 16 :, :] = jnp.zeros((16, HALF), BF16)
        wh[k, :VOC, :] = raw[k]
        for i in range(NZ):
            wt[k, i * PIECE : (i + 1) * PIECE, :] = wh[k, :, i * PIECE : (i + 1) * PIECE].T
    arrived(middle_y)
    middle_x = [same(buf.at[:, x, z, :, middle, :], at_x(wrap(x + off, NX))) for off in (2, 1, 3)]
    arrived(first_z)
    left_y0.start()
    right_x0.start()
    arrived(middle_x)
    along_z(0)
    left_y0.forward()
    right_x0.forward()
    arrived(last_z)
    left_y1.start()
    right_x1.start()
    left_y0.near()
    left_y0.far()
    left_x0.start()
    right_x0.near()
    right_x0.far()
    right_y0.start()
    along_z(1)
    left_y1.forward()
    right_x1.forward()
    left_x0.forward()
    right_y0.forward()
    along_z(2)
    left_y1.near()
    left_y1.far()
    left_x1.start()
    right_x1.near()
    right_x1.far()
    right_y1.start()
    lane = lax.broadcasted_iota(jnp.int32, (1, VPAD), 1)

    def multiply(blocks, rows):
        count = rows[1]
        lhs = [
            jnp.concatenate(
                [buf[yy, xx, k // 2, k % 2, rows[0] : rows[0] + count, :] for yy, xx in blocks],
                axis=0,
            )
            for k in range(2 * NZ)
        ]
        values = jnp.concatenate(lhs, axis=1)
        power = jnp.zeros((len(blocks) * count, 128), F32)
        for k in range(2 * NZ):
            wide = lhs[k].astype(F32)
            power = power + wide * wide * inv_gain[k : k + 1, :]
        power = jnp.sum(power, axis=1, keepdims=True)
        for ref, core in ((part, mate), (own, c)):
            product = jnp.dot(values, wt[core], preferred_element_type=F32)
            product = jnp.where(lane == VOC, power, product)
            for i, (yy, xx) in enumerate(blocks):
                ref[yy * NX + xx, rows[0] : rows[0] + count, :] = product[
                    i * count : (i + 1) * count, :
                ]
        swaps = []
        for yy, xx in blocks:
            at = yy * NX + xx
            span = pl.ds(*rows)
            swaps.append(wires.send(part.at[at, span, :], got.at[at, span, :], sibling))
        return swaps

    def finish(block, rows):
        at, span = block[0] * NX + block[1], slice(rows[0], rows[0] + rows[1])
        total = own[at, span, :] + got[at, span, :]
        logits = total * lax.rsqrt(total[:, VOC : VOC + 1] / D + 1e-05)
        own[at, span, :] = logits
        held = jnp.where(lane < VOC, logits, -jnp.inf)
        peak = jnp.max(held, axis=1, keepdims=True)
        mass = jnp.sum(jnp.exp(held - peak), axis=1, keepdims=True)
        return at, peak + jnp.log(mass)

    def place(count, shift):
        shape = (count, 128)
        row = lax.broadcasted_iota(jnp.int32, shape, 0)
        return lax.broadcasted_iota(jnp.int32, shape, 1) == row + shift

    def as_lanes(column, shift):
        return jnp.sum(jnp.where(place(column.shape[0], shift), column, 0.0), axis=0, keepdims=True)

    def as_column(lanes, count, shift):
        wide = jnp.broadcast_to(lanes, (count, 128))
        return jnp.sum(jnp.where(place(count, shift), wide, 0.0), axis=1, keepdims=True)

    def publish(at, rows, total):
        out_rows = slice(at * ROWS + rows[0], at * ROWS + rows[0] + rows[1])
        logits = own[at, rows[0] : rows[0] + rows[1], :]
        result[out_rows, :] = (logits - total)[:, :VOC].astype(BF16)
        leave(result.at[out_rows, :], out_ref.at[out_rows, :])

    def spread(value, mates, inbox):
        return [wires.send(value, inbox.at[i], other) for i, other in enumerate(mates)]

    def join(value, inbox):
        return log_add([value[...]] + [inbox[i] for i in range(inbox.shape[0])])

    near_y, near_x = [y, wrap(y + 1, NY), wrap(y + 3, NY)], [x, wrap(x + 1, NX), wrap(x + 3, NX)]
    far_y, far_x = wrap(y + 2, NY), wrap(x + 2, NX)
    near_blocks = [(yy, xx) for yy in near_y for xx in near_x]
    far_blocks = [(yy, far_x) for yy in near_y + [far_y]] + [(far_y, xx) for xx in near_x]
    lines = [[(yy, xx) for xx in range(NX)] for yy in range(NY)]
    def finish_first(blocks, swaps):
        for block, copy in zip(blocks, swaps):
            copy.wait_recv()
            at, column = finish(block, FIRST)
            lse_own[pl.ds(at, 1), :] = as_lanes(column, FIRST[0])

    left_x0.near()
    right_y0.near()
    near_first = []
    for i in range(3):
        near_first += multiply(near_blocks[3 * i : 3 * i + 3], FIRST)
    along_z(3)
    left_x0.far()
    right_y0.far()
    far_first = multiply(far_blocks[:4], FIRST)
    left_x1.forward()
    right_y1.forward()
    far_first += multiply(far_blocks[4:], FIRST)
    finish_first(near_blocks, near_first)
    finish_first(far_blocks, far_first)
    late_own[...] = jnp.zeros(late_own.shape, F32)

    def finish_last(blocks, swaps):
        for block, copy in zip(blocks, swaps):
            copy.wait_recv()
            at, column = finish(block, LAST)
            row = pl.ds(at // PER_ROW, 1)
            late_own[row, :] = late_own[row, :] + as_lanes(column, lax.rem(at, PER_ROW) * LAST[1])

    left_x1.near()
    right_y1.near()
    near_swaps = multiply(near_blocks, LAST)
    for copies in slabs[-1]:
        arrived(copies)
    swaps_middle = [multiply(line, MIDDLE) for line in lines]
    left_x1.far()
    right_y1.far()
    far_swaps = multiply(far_blocks, LAST)
    for line, swaps in zip(lines, swaps_middle):
        arrived(swaps)
        for block in line:
            at, column = finish(block, MIDDLE)
            lse_own[at : at + 1, :] = lse_own[at : at + 1, :] + as_lanes(column, MIDDLE[0])
    early_round = spread(lse_own, tensor_mates, lse_t)
    finish_last(near_blocks, near_swaps)
    finish_last(far_blocks, far_swaps)

    late_round = spread(late_own, tensor_mates, late_t)
    arrived(early_round)
    lse_mid[...] = join(lse_own, lse_t)
    early_round = spread(lse_mid, dp_mates, lse_d)
    arrived(late_round)
    late_mid[...] = join(late_own, late_t)
    late_round = spread(late_mid, dp_mates, late_d)
    arrived(early_round)
    early_total = join(lse_mid, lse_d)
    for at in range(NDP):
        publish(at, (0, EARLY), as_column(early_total[at : at + 1, :], EARLY, 0))
    arrived(late_round)
    late_total = join(late_mid, late_d)
    for at in range(NDP):
        row = late_total[at // PER_ROW : at // PER_ROW + 1, :]
        publish(at, LAST, as_column(row, LAST[1], (at % PER_ROW) * LAST[1]))
    for copy in outs:
        copy.wait()
    wires.close()


N_WIRES = 300
PARTS = 4


def step_call(args):
    hbm = pl.BlockSpec(memory_space=pl.ANY)
    return pl.pallas_call(
        step_kernel,
        out_shape=(
            jax.ShapeDtypeStruct((NDP * ROWS, VOC), BF16),
            jax.ShapeDtypeStruct((ROWS, NSTATE, CH), BF16),
        ),
        in_specs=[hbm] * len(args),
        out_specs=(hbm, hbm),
        scratch_shapes=[
            pltpu.VMEM((ROWS, CH), BF16),
            pltpu.VMEM((ROWS, CH), BF16),
            pltpu.VMEM((3, ROWS, CH), BF16),
            pltpu.VMEM((4, CH), F32),
            pltpu.VMEM((4, 128), F32),
            pltpu.VMEM((PROJ, CH), BF16),
            pltpu.VMEM((RANK, CH), BF16),
            pltpu.VMEM((4, 128), F32),
            pltpu.VMEM((NSTATE, CH), F32),
            pltpu.VMEM((4, 128), F32),
            pltpu.VMEM((ROWS, NSTATE, CH), BF16),
            pltpu.VMEM((D // 128, 128), F32),
            pltpu.VMEM((ROWS, CH), BF16),
            pltpu.VMEM((ROWS + 8, PROJ), F32),
            pltpu.VMEM((NT, 8, PROJ), BF16),
            pltpu.VMEM((NT - 1, 8, PROJ), BF16),
            pltpu.VMEM((NT, 8, PROJ), BF16),
            pltpu.VMEM((ROWS, CH), F32),
            pltpu.VMEM((NC, CH, HALF), BF16),
            pltpu.VMEM((NC, VOC, HALF), BF16),
            pltpu.VMEM((NC, VPAD, HALF), BF16),
            pltpu.VMEM((NC, ROWS, CH), BF16),
            pltpu.VMEM((ROWS, PIECE), BF16),
            pltpu.VMEM((2 * NZ, 128), F32),
            pltpu.VMEM((NZ, ROWS, PIECE), BF16),
            pltpu.VMEM((NZ, ROWS, PIECE), BF16),
            pltpu.VMEM((NY, NX, NZ, 2, ROWS, 128), BF16),
            pltpu.VMEM((NDP, ROWS, VPAD), F32),
            pltpu.VMEM((NDP, ROWS, VPAD), F32),
            pltpu.VMEM((NDP, ROWS, VPAD), F32),
            pltpu.VMEM((NDP, 128), F32),
            pltpu.VMEM((NT - 1, NDP, 128), F32),
            pltpu.VMEM((NDP, 128), F32),
            pltpu.VMEM((NDP - 1, NDP, 128), F32),
            pltpu.VMEM((NDP // PER_ROW, 128), F32),
            pltpu.VMEM((NT - 1, NDP // PER_ROW, 128), F32),
            pltpu.VMEM((NDP // PER_ROW, 128), F32),
            pltpu.VMEM((NDP - 1, NDP // PER_ROW, 128), F32),
            pltpu.VMEM((ROWS, PIECE), F32),
            pltpu.VMEM((ROWS, NSTATE, CH), BF16),
            pltpu.VMEM((NDP * ROWS, VOC), BF16),
            pltpu.VMEM((NC, HALF, VPAD), BF16),
            pltpu.SemaphoreType.DMA((N_WIRES,)),
            pltpu.SemaphoreType.DMA((N_WIRES,)),
            pltpu.SemaphoreType.DMA((64,)),
        ],
        compiler_params=pltpu.CompilerParams(
            collective_id=0, has_side_effects=True, vmem_limit_bytes=60 * 2**20
        ),
        name="step",
    )(*args)


def deliver_kernel(*refs):
    sources, targets, stages, sems = refs[:2], refs[2:4], refs[4:6], refs[6]
    pairs = []
    for src, stage, dst in zip(sources, stages, targets):
        size = src.shape[0] // PARTS
        for i in range(PARTS):
            rows = pl.ds(i * size, size)
            at = 2 * len(pairs)
            inward = pltpu.make_async_copy(src.at[rows], stage.at[rows], sems.at[at])
            outward = pltpu.make_async_copy(stage.at[rows], dst.at[rows], sems.at[at + 1])
            inward.start()
            pairs.append((inward, outward))
    for inward, outward in pairs:
        inward.wait()
        outward.start()
    for inward, outward in pairs:
        outward.wait()


def deliver(arrays):
    hbm = pl.BlockSpec(memory_space=pl.ANY)
    return pl.pallas_call(
        deliver_kernel,
        out_shape=tuple(jax.ShapeDtypeStruct(a.shape, a.dtype) for a in arrays),
        in_specs=[hbm] * 2,
        out_specs=(hbm, hbm),
        scratch_shapes=[pltpu.VMEM(a.shape, a.dtype) for a in arrays]
        + [pltpu.SemaphoreType.DMA((4 * PARTS,))],
        compiler_params=pltpu.CompilerParams(vmem_limit_bytes=60 * 2**20),
        name="deliver",
    )(*arrays)


def on_device(
    residual,
    x_in,
    z_in,
    conv_state,
    conv_weight,
    conv_bias,
    xproj_weight,
    dtproj_weight,
    dt_bias,
    a_log,
    skip_d,
    ssm_state,
    out_weight,
    norm_gain,
    head_weight,
):
    outs = step_call(
        (
            residual,
            x_in,
            z_in,
            conv_state,
            conv_weight,
            conv_bias.reshape(-1, 128),
            xproj_weight.T,
            dtproj_weight,
            dt_bias.reshape(-1, 128),
            a_log,
            skip_d.reshape(-1, 128),
            ssm_state,
            out_weight,
            norm_gain.reshape(-1, 128),
            head_weight,
        )
    )
    return deliver(outs)


def solution(mesh):
    torus = Mesh(mesh.devices.reshape(4, 4, 8, 2), ("dp_0", "dp_1", "tensor_0", "tensor_1"))
    placed = (
        P(DP, None),
        P(DP, TENSOR),
        P(DP, TENSOR),
        P(None, DP, TENSOR),
        P(None, TENSOR),
        P(TENSOR),
        P(TENSOR, None),
        P(None, TENSOR),
        P(TENSOR),
        P(None, TENSOR),
        P(TENSOR),
        P(DP, None, TENSOR),
        P(TENSOR, None),
        P(),
        P(DP_TENSOR, None),
    )
    return jax.shard_map(
        on_device,
        mesh=torus,
        in_specs=placed,
        out_specs=(P(None, DP_TENSOR), P(DP, None, TENSOR)),
        check_vma=False,
    )
```
